512 devices in a mesh: dp: 16 (over y, z_lo), ctx: 32 (over x, z_hi, core).
Axes of the slice: x: 4, y: 4, z: 16 (z_hi: 4, z_lo: 4; z = z_hi * 4 + z_lo), core: 2. Of those that a mesh axis runs over, the one named last changes fastest.
Arguments:
- queries: bfloat16 [16, 4096, 512], P('dp', 'ctx'), may hold values from -6 to 6
- keys: bfloat16 [16, 4096, 512], P('dp', 'ctx'), may hold values from -6 to 6
- values: bfloat16 [16, 4096, 512], P('dp', 'ctx'), may hold values from -6 to 6
- grad_out: bfloat16 [16, 4096, 512], P('dp', 'ctx'), may hold values from -6 to 6
- filter_taps: float32 [4096, 512], P('ctx'), may hold values from -0.125 to 0.125
Outputs:
- conv_out: bfloat16 [16, 4096, 512], P('dp', 'ctx')
- grad_queries: bfloat16 [16, 4096, 512], P('dp', 'ctx')
- grad_keys: bfloat16 [16, 4096, 512], P('dp', 'ctx')
- grad_values: bfloat16 [16, 4096, 512], P('dp', 'ctx')
- grad_filter: float32 [4096, 512], P('ctx')
The draws below stay inside these ranges and needn't reach their ends.
All inputs are finite; a program needn't handle non-finite values.
Results may differ from the reference program's by a relative error of at most 0.0023.
Values sent between devices are 32-bit elements; how exact they have to be, the bound alone decides.
No kernel may reach another device: no remote copies, remote signals or barrier semaphores. Data moves between devices by JAX's collectives and lax.ppermute only.
A program may use at most 64 MiB of HBM per device.

```python
import math
import jax
import jax.numpy as jnp
from jax import lax

C = 512
SEQS = 16
LEN = 4096


def steps_of(rng, dims, pieces, smallest, high):
    loudness = 1.0
    for position, blocks in pieces:
        steps = jax.random.uniform(jax.random.fold_in(jax.random.fold_in(rng, 6), position), (blocks,), jnp.float32, smallest / len(pieces), high / len(pieces))
        loudness = loudness * jnp.repeat(jnp.exp(steps), dims[position] // blocks).reshape((-1,) + (1,) * (len(dims) - 1 - position))
    return loudness


def bell_draw(own_key, shape, width, limit, cuts=(), kind=jnp.bfloat16):
    entries = width * jax.random.normal(own_key, shape, jnp.float32)
    if cuts:
        entries = entries * steps_of(own_key, shape, cuts, -0.22, 0.18)
    return jnp.clip(entries, -limit, limit).astype(kind)


def setup_inputs(seed: int = 0) -> dict:
    splits = jax.random.split(jax.random.key(seed), 6)
    queries = bell_draw(splits[0], (SEQS, LEN, C), 1.0, 6.0, ((0, 16), (1, 32)))
    keys = bell_draw(splits[1], (SEQS, LEN, C), 1.0, 6.0, ((0, 16), (1, 32)))
    values = bell_draw(splits[2], (SEQS, LEN, C), 1.0, 6.0, ((0, 16), (1, 32)))
    grad_out = bell_draw(splits[3], (SEQS, LEN, C), 1.0, 6.0, ((0, 16), (1, 32)))
    filter_taps = bell_draw(splits[4], (LEN, C), (LEN // 2) ** -0.5, 0.125, ((0, 32),), jnp.float32)
    return dict(queries=queries, keys=keys, values=values, grad_out=grad_out, filter_taps=filter_taps)


def reference(queries, keys, values, grad_out, filter_taps):
    padded_len = 2 * LEN
    filter_freq = jnp.fft.rfft(filter_taps, n=padded_len, axis=0)

    def per_sequence(items):
        query_rows, key_rows, value_rows, grad_rows = items
        query_f = query_rows.astype(jnp.float32)
        key_f = key_rows.astype(jnp.float32)
        value_f = value_rows.astype(jnp.float32)
        grad_f = grad_rows.astype(jnp.float32)
        gated = key_f * value_f
        grad_s = grad_f * query_f
        gated_freq = jnp.fft.rfft(gated, n=padded_len, axis=0)
        grad_freq = jnp.fft.rfft(grad_s, n=padded_len, axis=0)
        conv_s = jnp.fft.irfft(filter_freq * gated_freq, n=padded_len, axis=0)[:LEN].astype(gated.dtype)
        grad_z = jnp.fft.irfft(jnp.conj(filter_freq) * grad_freq, n=padded_len, axis=0)[:LEN].astype(gated.dtype)
        lag_grad = jnp.fft.irfft(grad_freq * jnp.conj(gated_freq), n=padded_len, axis=0)[:LEN].astype(gated.dtype)
        conv_out = (query_f * conv_s).astype(jnp.bfloat16)
        grad_queries = (grad_f * conv_s).astype(jnp.bfloat16)
        grad_keys = (grad_z * value_f).astype(jnp.bfloat16)
        grad_values = (grad_z * key_f).astype(jnp.bfloat16)
        return (conv_out, grad_queries, grad_keys, grad_values, lag_grad)
    conv_out, grad_queries, grad_keys, grad_values, lag_all = lax.map(per_sequence, (queries, keys, values, grad_out))
    grad_filter = lax.optimization_barrier(jnp.sum(lag_all, axis=0)) * (1.0 / math.sqrt(SEQS * LEN))
    return (conv_out, grad_queries, grad_keys, grad_values, grad_filter)
```

```python
import math

import jax
import jax.numpy as jnp
import ml_dtypes
import numpy as np
from jax import lax
from jax.experimental import pallas as pl
from jax.experimental.pallas import tpu as pltpu
from jax.sharding import Mesh
from jax.sharding import PartitionSpec as P

BLK = 128
NB = 32
CG = 4
KH = 40
IN_ROWS = 2 * CG + 1
OUT_ROWS = 3 * CG
PERIOD = 2 * NB * BLK
VMEM = pl.BlockSpec(memory_space=pltpu.VMEM)
PARAMS = pltpu.CompilerParams(vmem_limit_bytes=40 * 1024 * 1024)


def high_low(table):
    high = table.astype(ml_dtypes.bfloat16)
    low = (table - high.astype(np.float64)).astype(ml_dtypes.bfloat16)
    return high, low


def tables():
    k1 = np.arange(KH)
    used = (k1 <= NB)[:, None]
    block = np.arange(NB)
    angle = 2.0 * np.pi * ((k1[:, None] * block[None, :]) % (2 * NB)) / (2 * NB)
    mix = np.concatenate([np.cos(angle) * used, -np.sin(angle) * used], 0)
    high, low = high_low(mix)
    forward_mix = np.concatenate([high, high, low], 1)
    weight = np.where((k1 == 0) | (k1 == NB), 1.0, 2.0)[:, None] * used / PERIOD
    back = np.concatenate([np.cos(angle) * weight, -np.sin(angle) * weight], 0).T
    high, low = high_low(back)
    inverse_mix = np.concatenate([high, high, low], 1)
    offset = np.arange(BLK)
    turn = 2.0 * np.pi * (k1[:, None] * offset[None, :]) / PERIOD
    cos_turn = (np.cos(turn) * used).astype(np.float32)
    sin_turn = (np.sin(turn) * used).astype(np.float32)
    full = 2.0 * np.pi * ((offset[:, None] * offset[None, :]) % BLK) / BLK
    cos, sin = np.cos(full), np.sin(full)
    high, low = high_low(np.block([[cos, -sin], [sin, cos]]))
    forward_full = np.concatenate([high, high, low], 0)
    high, low = high_low(np.block([[cos, sin], [-sin, cos]]))
    inverse_full = np.concatenate([high, high, low], 0)
    return forward_mix, inverse_mix, cos_turn, sin_turn, forward_full, inverse_full


def split(value):
    high = value.astype(jnp.bfloat16)
    low = (value - high.astype(jnp.float32)).astype(jnp.bfloat16)
    return high, low


def dot(left, right):
    return jnp.dot(left, right, preferred_element_type=jnp.float32)


def mix_rows(table, operand):
    high, low = split(operand)
    return dot(table, jnp.concatenate([high, low, high], 0))


def full_transform(operand, table_ref):
    high, low = split(operand)
    return dot(jnp.concatenate([high, low, high], 1), table_ref[...])


def spectra(blocks, mix, cos_turn, sin_turn, full_ref):
    mixed = mix_rows(mix, jnp.concatenate(blocks, 1))
    turned = []
    for index in range(len(blocks)):
        lanes = slice(index * BLK, (index + 1) * BLK)
        real, imag = mixed[:KH, lanes], mixed[KH:, lanes]
        turned.append(
            jnp.concatenate(
                [real * cos_turn + imag * sin_turn, imag * cos_turn - real * sin_turn], 1
            )
        )
    return full_transform(jnp.concatenate(turned, 0), full_ref)


def positions(spectrum, count, mix, cos_turn, sin_turn, full_ref):
    back = full_transform(spectrum, full_ref)
    columns = []
    for index in range(count):
        rows = slice(index * KH, (index + 1) * KH)
        real, imag = back[rows, :BLK], back[rows, BLK:]
        columns.append(
            jnp.concatenate(
                [real * cos_turn - imag * sin_turn, imag * cos_turn + real * sin_turn], 0
            )
        )
    return mix_rows(mix, jnp.concatenate(columns, 1))


def send_kernel(query_ref, key_ref, value_ref, grad_ref, taps_ref, out_ref):
    group = lax.axis_index("zl")
    for part in range(CG):
        lanes = slice(part * BLK, (part + 1) * BLK)
        gated = key_ref[0, :, lanes].astype(jnp.float32) * value_ref[0, :, lanes].astype(jnp.float32)
        grad_s = grad_ref[0, :, lanes].astype(jnp.float32) * query_ref[0, :, lanes].astype(jnp.float32)
        out_ref[pl.ds(part, BLK, IN_ROWS), :] = gated.T
        out_ref[pl.ds(CG + part, BLK, IN_ROWS), :] = grad_s.T
    own = taps_ref[:, pl.ds(pl.multiple_of(group * BLK, BLK), BLK)]
    out_ref[pl.ds(2 * CG, BLK, IN_ROWS), :] = own.T


def forward_kernel(
    rows_ref, mix_ref, cos_ref, sin_ref, full_ref, inv_mix_ref, inv_full_ref, conv_ref, back_ref, lag_ref
):
    mix, cos_turn, sin_turn = mix_ref[...], cos_ref[...], sin_ref[...]
    wide = CG * KH

    def block(seq, row):
        return rows_ref[pl.ds(seq * NB * IN_ROWS + row, NB, IN_ROWS), :]

    taps = spectra([block(part, 2 * CG) for part in range(CG)], mix, cos_turn, sin_turn, full_ref)
    taps_re, taps_im = taps[:, :BLK], taps[:, BLK:]
    lag = None
    for seq in range(CG):
        both = spectra([block(seq, row) for row in range(2 * CG)], mix, cos_turn, sin_turn, full_ref)
        gated_re, gated_im = both[:wide, :BLK], both[:wide, BLK:]
        grad_re, grad_im = both[wide:, :BLK], both[wide:, BLK:]
        rows = slice(seq * wide, (seq + 1) * wide)
        conv_ref[rows, :BLK] = taps_re * gated_re - taps_im * gated_im
        conv_ref[rows, BLK:] = taps_re * gated_im + taps_im * gated_re
        back_ref[rows, :BLK] = taps_re * grad_re + taps_im * grad_im
        back_ref[rows, BLK:] = taps_re * grad_im - taps_im * grad_re
        term = jnp.concatenate(
            [grad_re * gated_re + grad_im * gated_im, grad_im * gated_re - grad_re * gated_im], 1
        )
        lag = term if lag is None else lag + term
    timed = positions(lag, CG, inv_mix_ref[...], cos_turn, sin_turn, inv_full_ref)
    for copy in range(4):
        for part in range(CG):
            first = (copy * CG + part) * NB
            lag_ref[first : first + NB, :] = timed[:, part * BLK : (part + 1) * BLK]


def inverse_kernel(conv_ref, back_ref, cos_ref, sin_ref, mix_ref, full_ref, out_ref):
    mix, cos_turn, sin_turn = mix_ref[...], cos_ref[...], sin_ref[...]
    wide = CG * KH
    for seq in range(CG):
        rows = slice(seq * wide, (seq + 1) * wide)
        for which, ref in enumerate((conv_ref, back_ref)):
            timed = positions(ref[rows, :], CG, mix, cos_turn, sin_turn, full_ref)
            for part in range(CG):
                first = seq * NB * OUT_ROWS + which * CG + part
                out_ref[pl.ds(first, NB, OUT_ROWS), :] = timed[:, part * BLK : (part + 1) * BLK]


def lag_kernel(parts_ref, held_ref, out_ref):
    del held_ref
    own = CG * NB
    total = parts_ref[:own, :] + parts_ref[own : 2 * own, :]
    total = total + (parts_ref[2 * own : 3 * own, :] + parts_ref[3 * own :, :])
    for seq in range(CG):
        for part in range(CG):
            first = seq * NB * OUT_ROWS + 2 * CG + part
            out_ref[pl.ds(first, NB, OUT_ROWS), :] = total[part * NB : (part + 1) * NB, :]


def finish_kernel(
    scale, rows_ref, query_ref, key_ref, value_ref, grad_ref, conv_out_ref, gq_ref, gk_ref, gv_ref, gf_ref
):
    for part in range(CG):
        lanes = slice(part * BLK, (part + 1) * BLK)
        conv_s = rows_ref[pl.ds(part, BLK, OUT_ROWS), :].T
        grad_z = rows_ref[pl.ds(CG + part, BLK, OUT_ROWS), :].T
        lag = rows_ref[pl.ds(2 * CG + part, BLK, OUT_ROWS), :].T
        conv_out_ref[0, :, lanes] = (query_ref[0, :, lanes].astype(jnp.float32) * conv_s).astype(jnp.bfloat16)
        gq_ref[0, :, lanes] = (grad_ref[0, :, lanes].astype(jnp.float32) * conv_s).astype(jnp.bfloat16)
        gk_ref[0, :, lanes] = (grad_z * value_ref[0, :, lanes].astype(jnp.float32)).astype(jnp.bfloat16)
        gv_ref[0, :, lanes] = (grad_z * key_ref[0, :, lanes].astype(jnp.float32)).astype(jnp.bfloat16)
        gf_ref[:, lanes] = lag * scale


def call(kernel, out_shape, count, **kwargs):
    single = not isinstance(out_shape, (tuple, list))
    return pl.pallas_call(
        kernel,
        out_shape=out_shape,
        in_specs=[VMEM] * count,
        out_specs=VMEM if single else [VMEM] * len(out_shape),
        compiler_params=PARAMS,
        **kwargs,
    )


def f32(*shape):
    return jax.ShapeDtypeStruct(shape, jnp.float32)


def exchange(rows, per):
    peers = 4 * NB
    moved = lax.all_to_all(rows.reshape(peers, per, 1, BLK), ("zl", "ctx"), 0, 0, tiled=True)
    return moved.reshape(peers * per, BLK)


def local(queries, keys, values, grad_out, filter_taps):
    forward_mix, inverse_mix, cos_turn, sin_turn, forward_full, inverse_full = (
        jnp.asarray(t) for t in tables()
    )
    sent = call(send_kernel, f32(4 * NB * IN_ROWS, BLK), 5)(queries, keys, values, grad_out, filter_taps)
    rows = exchange(sent, IN_ROWS)
    wide = CG * CG * KH
    conv, back, lag = call(forward_kernel, (f32(wide, 2 * BLK), f32(wide, 2 * BLK), f32(4 * CG * NB, BLK)), 7)(
        rows, forward_mix, cos_turn, sin_turn, forward_full, inverse_mix, inverse_full
    )
    parts = lax.all_to_all(lag.reshape(4, CG * NB, BLK), "y", 0, 0, tiled=True).reshape(4 * CG * NB, BLK)
    timed = call(inverse_kernel, f32(4 * NB * OUT_ROWS, BLK), 6)(
        conv, back, cos_turn, sin_turn, inverse_mix, inverse_full
    )
    timed = call(lag_kernel, f32(4 * NB * OUT_ROWS, BLK), 2, input_output_aliases={1: 0})(parts, timed)
    returned = exchange(timed, OUT_ROWS)
    scale = 1.0 / math.sqrt(16 * NB * BLK)
    shape = jax.ShapeDtypeStruct(queries.shape, jnp.bfloat16)

    def finish(*refs):
        finish_kernel(scale, *refs)

    return tuple(
        call(finish, (shape, shape, shape, shape, f32(*filter_taps.shape)), 5)(
            returned, queries, keys, values, grad_out
        )
    )


def solution(mesh):
    split_mesh = Mesh(mesh.devices.reshape(4, 4, 32), ("y", "zl", "ctx"))
    whole = P(("y", "zl"), "ctx", None)
    return jax.shard_map(
        local,
        mesh=split_mesh,
        in_specs=(whole, whole, whole, whole, P("ctx", None)),
        out_specs=(whole, whole, whole, whole, P("ctx", None)),
        check_vma=False,
    )
```

```python
import math

import jax
import jax.numpy as jnp
import ml_dtypes
import numpy as np
from jax import lax
from jax.experimental import pallas as pl
from jax.experimental.pallas import tpu as pltpu
from jax.sharding import Mesh
from jax.sharding import PartitionSpec as P

BLK = 128
NB = 32
CG = 4
KH = 40
IN_ROWS = 2 * CG + 1
OUT_ROWS = 3 * CG
PERIOD = 2 * NB * BLK
VMEM = pl.BlockSpec(memory_space=pltpu.VMEM)
HBM = pl.BlockSpec(memory_space=pltpu.HBM)
PARAMS = pltpu.CompilerParams(vmem_limit_bytes=40 * 1024 * 1024)


def high_low(table):
    high = table.astype(ml_dtypes.bfloat16)
    low = (table - high.astype(np.float64)).astype(ml_dtypes.bfloat16)
    return high, low


def tables():
    k1 = np.arange(KH)
    used = (k1 <= NB)[:, None]
    block = np.arange(NB)
    angle = 2.0 * np.pi * ((k1[:, None] * block[None, :]) % (2 * NB)) / (2 * NB)
    mix = np.concatenate([np.cos(angle) * used, -np.sin(angle) * used], 0)
    high, low = high_low(mix)
    forward_mix = np.concatenate([high, high, low], 1)
    weight = np.where((k1 == 0) | (k1 == NB), 1.0, 2.0)[:, None] * used / PERIOD
    back = np.concatenate([np.cos(angle) * weight, -np.sin(angle) * weight], 0).T
    high, low = high_low(back)
    inverse_mix = np.concatenate([high, high, low], 1)
    offset = np.arange(BLK)
    turn = 2.0 * np.pi * (k1[:, None] * offset[None, :]) / PERIOD
    cos_turn = (np.cos(turn) * used).astype(np.float32)
    sin_turn = (np.sin(turn) * used).astype(np.float32)
    full = 2.0 * np.pi * ((offset[:, None] * offset[None, :]) % BLK) / BLK
    cos, sin = np.cos(full), np.sin(full)
    high, low = high_low(np.block([[cos, -sin], [sin, cos]]))
    forward_full = np.concatenate([high, high, low], 0)
    high, low = high_low(np.block([[cos, sin], [-sin, cos]]))
    inverse_full = np.concatenate([high, high, low], 0)
    return forward_mix, inverse_mix, cos_turn, sin_turn, forward_full, inverse_full


def split(value):
    high = value.astype(jnp.bfloat16)
    low = (value - high.astype(jnp.float32)).astype(jnp.bfloat16)
    return high, low


def dot(left, right):
    return jnp.dot(left, right, preferred_element_type=jnp.float32)


def mix_rows(table, operand):
    high, low = split(operand)
    return dot(table, jnp.concatenate([high, low, high], 0))


def full_transform(operand, table_ref):
    high, low = split(operand)
    return dot(jnp.concatenate([high, low, high], 1), table_ref[...])


def spectra(blocks, mix, cos_turn, sin_turn, full_ref):
    mixed = mix_rows(mix, jnp.concatenate(blocks, 1))
    turned = []
    for index in range(len(blocks)):
        lanes = slice(index * BLK, (index + 1) * BLK)
        real, imag = mixed[:KH, lanes], mixed[KH:, lanes]
        turned.append(
            jnp.concatenate(
                [real * cos_turn + imag * sin_turn, imag * cos_turn - real * sin_turn], 1
            )
        )
    return full_transform(jnp.concatenate(turned, 0), full_ref)


def positions(spectrum, count, mix, cos_turn, sin_turn, full_ref):
    back = full_transform(spectrum, full_ref)
    columns = []
    for index in range(count):
        rows = slice(index * KH, (index + 1) * KH)
        real, imag = back[rows, :BLK], back[rows, BLK:]
        columns.append(
            jnp.concatenate(
                [real * cos_turn - imag * sin_turn, imag * cos_turn + real * sin_turn], 0
            )
        )
    return mix_rows(mix, jnp.concatenate(columns, 1))


def send_kernel(query_ref, key_ref, value_ref, grad_ref, taps_ref, out_ref, query, key, value, grad, taps, sems):
    group = lax.axis_index("zl")
    own = taps_ref.at[:, pl.ds(pl.multiple_of(group * BLK, BLK), BLK)]
    pairs = ((key_ref, key), (value_ref, value), (grad_ref, grad), (query_ref, query), (own, taps))
    copies = [pltpu.make_async_copy(src, dst, sems.at[index]) for index, (src, dst) in enumerate(pairs)]
    for copy in copies:
        copy.start()
    copies[0].wait()
    copies[1].wait()
    for part in range(CG):
        lanes = slice(part * BLK, (part + 1) * BLK)
        gated = key[0, :, lanes].astype(jnp.float32) * value[0, :, lanes].astype(jnp.float32)
        out_ref[pl.ds(part, BLK, IN_ROWS), :] = gated.T
    copies[2].wait()
    copies[3].wait()
    for part in range(CG):
        lanes = slice(part * BLK, (part + 1) * BLK)
        grad_s = grad[0, :, lanes].astype(jnp.float32) * query[0, :, lanes].astype(jnp.float32)
        out_ref[pl.ds(CG + part, BLK, IN_ROWS), :] = grad_s.T
    copies[4].wait()
    out_ref[pl.ds(2 * CG, BLK, IN_ROWS), :] = taps[...].T


def block(rows_ref, seq, row):
    return rows_ref[pl.ds(seq * NB * IN_ROWS + row, NB, IN_ROWS), :]


def forward_kernel(
    rows_ref, mix_ref, cos_ref, sin_ref, full_ref, inv_mix_ref, inv_full_ref, gated_ref, grad_ref, lag_ref
):
    mix, cos_turn, sin_turn = mix_ref[...], cos_ref[...], sin_ref[...]
    wide = CG * KH
    lag = None
    for seq in range(CG):
        blocks = [block(rows_ref, seq, row) for row in range(2 * CG)]
        both = spectra(blocks, mix, cos_turn, sin_turn, full_ref)
        rows = slice(seq * wide, (seq + 1) * wide)
        gated_ref[rows, :] = both[:wide]
        grad_ref[rows, :] = both[wide:]
        gated_re, gated_im = both[:wide, :BLK], both[:wide, BLK:]
        grad_re, grad_im = both[wide:, :BLK], both[wide:, BLK:]
        term = jnp.concatenate(
            [grad_re * gated_re + grad_im * gated_im, grad_im * gated_re - grad_re * gated_im], 1
        )
        lag = term if lag is None else lag + term
    timed = positions(lag, CG, inv_mix_ref[...], cos_turn, sin_turn, inv_full_ref)
    for copy in range(4):
        for part in range(CG):
            first = (copy * CG + part) * NB
            lag_ref[first : first + NB, :] = timed[:, part * BLK : (part + 1) * BLK]


def inverse_kernel(
    rows_ref, gated_ref, grad_ref, mix_ref, cos_ref, sin_ref, full_ref, inv_mix_ref, inv_full_ref, out_ref
):
    mix, cos_turn, sin_turn = mix_ref[...], cos_ref[...], sin_ref[...]
    inv_mix = inv_mix_ref[...]
    wide = CG * KH
    taps = spectra([block(rows_ref, part, 2 * CG) for part in range(CG)], mix, cos_turn, sin_turn, full_ref)
    taps_re, taps_im = taps[:, :BLK], taps[:, BLK:]
    for seq in range(CG):
        rows = slice(seq * wide, (seq + 1) * wide)
        gated_re, gated_im = gated_ref[rows, :BLK], gated_ref[rows, BLK:]
        grad_re, grad_im = grad_ref[rows, :BLK], grad_ref[rows, BLK:]
        conv = jnp.concatenate(
            [taps_re * gated_re - taps_im * gated_im, taps_re * gated_im + taps_im * gated_re], 1
        )
        back = jnp.concatenate(
            [taps_re * grad_re + taps_im * grad_im, taps_re * grad_im - taps_im * grad_re], 1
        )
        timed = positions(jnp.concatenate([conv, back], 0), 2 * CG, inv_mix, cos_turn, sin_turn, inv_full_ref)
        for row in range(2 * CG):
            out_ref[pl.ds(seq * NB * 2 * CG + row, NB, 2 * CG), :] = timed[:, row * BLK : (row + 1) * BLK]


def join_kernel(shares_ref, timed_ref, out_ref):
    peers = CG * NB
    lag = shares_ref[:peers, :] + shares_ref[peers : 2 * peers, :]
    lag = lag + (shares_ref[2 * peers : 3 * peers, :] + shares_ref[3 * peers :, :])
    for row in range(2 * CG):
        out_ref[pl.ds(row, peers, OUT_ROWS), :] = timed_ref[pl.ds(row, peers, 2 * CG), :]
    for seq in range(CG):
        for part in range(CG):
            first = seq * NB * OUT_ROWS + 2 * CG + part
            out_ref[pl.ds(first, NB, OUT_ROWS), :] = lag[part * NB : (part + 1) * NB, :]


def finish_kernel(
    scale, rows_ref, query_ref, key_ref, value_ref, grad_ref, conv_out_ref, gq_ref, gk_ref, gv_ref, gf_ref
):
    for part in range(CG):
        lanes = slice(part * BLK, (part + 1) * BLK)
        conv_s = rows_ref[pl.ds(part, BLK, OUT_ROWS), :].T
        grad_z = rows_ref[pl.ds(CG + part, BLK, OUT_ROWS), :].T
        lag = rows_ref[pl.ds(2 * CG + part, BLK, OUT_ROWS), :].T
        conv_out_ref[0, :, lanes] = (query_ref[0, :, lanes].astype(jnp.float32) * conv_s).astype(jnp.bfloat16)
        gq_ref[0, :, lanes] = (grad_ref[0, :, lanes].astype(jnp.float32) * conv_s).astype(jnp.bfloat16)
        gk_ref[0, :, lanes] = (grad_z * value_ref[0, :, lanes].astype(jnp.float32)).astype(jnp.bfloat16)
        gv_ref[0, :, lanes] = (grad_z * key_ref[0, :, lanes].astype(jnp.float32)).astype(jnp.bfloat16)
        gf_ref[:, lanes] = lag * scale


def call(kernel, out_shape, count, space=VMEM, params=PARAMS, **kwargs):
    single = not isinstance(out_shape, (tuple, list))
    return pl.pallas_call(
        kernel,
        out_shape=out_shape,
        in_specs=[space] * count,
        out_specs=VMEM if single else [VMEM] * len(out_shape),
        compiler_params=params,
        **kwargs,
    )


def f32(*shape):
    return jax.ShapeDtypeStruct(shape, jnp.float32)


def exchange(rows, per):
    peers = CG * NB
    moved = lax.all_to_all(rows.reshape(peers, per, 1, BLK), ("zl", "ctx"), 0, 0, tiled=True)
    return moved.reshape(peers * per, BLK)


def local(queries, keys, values, grad_out, filter_taps):
    forward_mix, inverse_mix, cos_turn, sin_turn, forward_full, inverse_full = (
        jnp.asarray(t) for t in tables()
    )
    peers = CG * NB
    wide = CG * CG * KH
    scratch = [pltpu.VMEM(queries.shape, jnp.bfloat16)] * 4 + [
        pltpu.VMEM((BLK, BLK), jnp.float32),
        pltpu.SemaphoreType.DMA((5,)),
    ]
    sent = call(send_kernel, f32(peers * IN_ROWS, BLK), 5, HBM, None, scratch_shapes=scratch)(
        queries, keys, values, grad_out, filter_taps
    )
    rows = exchange(sent, IN_ROWS)
    gated, grad, lag = call(forward_kernel, (f32(wide, 2 * BLK), f32(wide, 2 * BLK), f32(4 * peers, BLK)), 7)(
        rows, forward_mix, cos_turn, sin_turn, forward_full, inverse_mix, inverse_full
    )
    shares = lax.all_to_all(lag.reshape(4, peers, BLK), "y", 0, 0, tiled=True).reshape(4 * peers, BLK)
    timed = call(inverse_kernel, f32(peers * 2 * CG, BLK), 9)(
        rows, gated, grad, forward_mix, cos_turn, sin_turn, forward_full, inverse_mix, inverse_full
    )
    joined = call(join_kernel, f32(peers * OUT_ROWS, BLK), 2)(shares, timed)
    returned = exchange(joined, OUT_ROWS)
    scale = 1.0 / math.sqrt(16 * NB * BLK)
    shape = jax.ShapeDtypeStruct(queries.shape, jnp.bfloat16)

    def finish(*refs):
        finish_kernel(scale, *refs)

    return tuple(
        call(finish, (shape, shape, shape, shape, f32(*filter_taps.shape)), 5)(
            returned, queries, keys, values, grad_out
        )
    )


def solution(mesh):
    split_mesh = Mesh(mesh.devices.reshape(4, 4, 32), ("y", "zl", "ctx"))
    whole = P(("y", "zl"), "ctx", None)
    return jax.shard_map(
        local,
        mesh=split_mesh,
        in_specs=(whole, whole, whole, whole, P("ctx", None)),
        out_specs=(whole, whole, whole, whole, P("ctx", None)),
        check_vma=False,
    )
```

```python
import functools
import math

import jax
import jax.numpy as jnp
import ml_dtypes
import numpy as np
from jax import lax
from jax.experimental import pallas as pl
from jax.experimental.pallas import tpu as pltpu
from jax.sharding import Mesh
from jax.sharding import PartitionSpec as P

BLK = 128
NB = 32
CG = 4
KH = 40
IN_ROWS = 2 * CG + 1
OUT_ROWS = 2 * CG + 1
PERIOD = 2 * NB * BLK
VMEM = pl.BlockSpec(memory_space=pltpu.VMEM)
HBM = pl.BlockSpec(memory_space=pltpu.HBM)
SMALL = pltpu.CompilerParams(vmem_limit_bytes=8 * 1024 * 1024)
PARAMS = pltpu.CompilerParams(vmem_limit_bytes=40 * 1024 * 1024)


def high_low(table):
    high = table.astype(ml_dtypes.bfloat16)
    low = (table - high.astype(np.float64)).astype(ml_dtypes.bfloat16)
    return high, low


def tables():
    k1 = np.arange(KH)
    used = (k1 <= NB)[:, None]
    block = np.arange(NB)
    angle = 2.0 * np.pi * ((k1[:, None] * block[None, :]) % (2 * NB)) / (2 * NB)
    mix = np.concatenate([np.cos(angle) * used, -np.sin(angle) * used], 0)
    high, low = high_low(mix)
    forward_mix = np.concatenate([high, high, low], 1)
    weight = np.where((k1 == 0) | (k1 == NB), 1.0, 2.0)[:, None] * used / PERIOD
    back = np.concatenate([np.cos(angle) * weight, -np.sin(angle) * weight], 0).T
    high, low = high_low(back)
    inverse_mix = np.concatenate([high, high, low], 1)
    offset = np.arange(BLK)
    turn = 2.0 * np.pi * (k1[:, None] * offset[None, :]) / PERIOD
    cos_turn = (np.cos(turn) * used).astype(np.float32)
    sin_turn = (np.sin(turn) * used).astype(np.float32)
    full = 2.0 * np.pi * ((offset[:, None] * offset[None, :]) % BLK) / BLK
    cos, sin = np.cos(full), np.sin(full)
    high, low = high_low(np.block([[cos, -sin], [sin, cos]]))
    forward_full = np.concatenate([high, high, low], 0)
    high, low = high_low(np.block([[cos, sin], [-sin, cos]]))
    inverse_full = np.concatenate([high, high, low], 0)
    return forward_mix, inverse_mix, cos_turn, sin_turn, forward_full, inverse_full


def split(value):
    high = value.astype(jnp.bfloat16)
    low = (value - high.astype(jnp.float32)).astype(jnp.bfloat16)
    return high, low


def dot(left, right):
    return jnp.dot(left, right, preferred_element_type=jnp.float32)


def mix_rows(table, operand):
    high, low = split(operand)
    return dot(table, jnp.concatenate([high, low, high], 0))


def full_transform(operand, table_ref):
    high, low = split(operand)
    return dot(jnp.concatenate([high, low, high], 1), table_ref[...])


def spectra(blocks, mix, cos_turn, sin_turn, full_ref):
    mixed = mix_rows(mix, jnp.concatenate(blocks, 1))
    turned = []
    for index in range(len(blocks)):
        lanes = slice(index * BLK, (index + 1) * BLK)
        real, imag = mixed[:KH, lanes], mixed[KH:, lanes]
        turned.append(
            jnp.concatenate(
                [real * cos_turn + imag * sin_turn, imag * cos_turn - real * sin_turn], 1
            )
        )
    return full_transform(jnp.concatenate(turned, 0), full_ref)


def positions(spectrum, count, mix, cos_turn, sin_turn, full_ref):
    back = full_transform(spectrum, full_ref)
    columns = []
    for index in range(count):
        rows = slice(index * KH, (index + 1) * KH)
        real, imag = back[rows, :BLK], back[rows, BLK:]
        columns.append(
            jnp.concatenate(
                [real * cos_turn - imag * sin_turn, imag * cos_turn + real * sin_turn], 0
            )
        )
    return mix_rows(mix, jnp.concatenate(columns, 1))


def send_kernel(query_ref, key_ref, value_ref, grad_ref, taps_ref, out_ref, query, key, value, grad, taps, sems):
    group = lax.axis_index("zl")
    own = taps_ref.at[:, pl.ds(pl.multiple_of(group * BLK, BLK), BLK)]
    pairs = ((key_ref, key), (value_ref, value), (grad_ref, grad), (query_ref, query), (own, taps))
    copies = [pltpu.make_async_copy(src, dst, sems.at[index]) for index, (src, dst) in enumerate(pairs)]
    for copy in copies:
        copy.start()
    copies[0].wait()
    copies[1].wait()
    for part in range(CG):
        lanes = slice(part * BLK, (part + 1) * BLK)
        gated = key[0, :, lanes].astype(jnp.float32) * value[0, :, lanes].astype(jnp.float32)
        out_ref[pl.ds(part, BLK, IN_ROWS), :] = gated.T
    copies[2].wait()
    copies[3].wait()
    for part in range(CG):
        lanes = slice(part * BLK, (part + 1) * BLK)
        grad_s = grad[0, :, lanes].astype(jnp.float32) * query[0, :, lanes].astype(jnp.float32)
        out_ref[pl.ds(CG + part, BLK, IN_ROWS), :] = grad_s.T
    copies[4].wait()
    out_ref[pl.ds(2 * CG, BLK, IN_ROWS), :] = taps[...].T


def block(rows_ref, seq, row):
    return rows_ref[pl.ds(seq * NB * IN_ROWS + row, NB, IN_ROWS), :]


def forward_kernel(
    rows_ref, mix_ref, cos_ref, sin_ref, full_ref, inv_mix_ref, inv_full_ref, gated_ref, grad_ref, lag_ref
):
    mix, cos_turn, sin_turn = mix_ref[...], cos_ref[...], sin_ref[...]
    wide = CG * KH
    lag = None
    for seq in range(CG):
        blocks = [block(rows_ref, seq, row) for row in range(2 * CG)]
        both = spectra(blocks, mix, cos_turn, sin_turn, full_ref)
        rows = slice(seq * wide, (seq + 1) * wide)
        gated_ref[rows, :] = both[:wide]
        grad_ref[rows, :] = both[wide:]
        gated_re, gated_im = both[:wide, :BLK], both[:wide, BLK:]
        grad_re, grad_im = both[wide:, :BLK], both[wide:, BLK:]
        term = jnp.concatenate(
            [grad_re * gated_re + grad_im * gated_im, grad_im * gated_re - grad_re * gated_im], 1
        )
        lag = term if lag is None else lag + term
    timed = positions(lag, CG, inv_mix_ref[...], cos_turn, sin_turn, inv_full_ref)
    for part in range(CG):
        lag_ref[part * NB : (part + 1) * NB, :] = timed[:, part * BLK : (part + 1) * BLK]


def inverse_kernel(
    rows_ref, gated_ref, grad_ref, mix_ref, cos_ref, sin_ref, full_ref, inv_mix_ref, inv_full_ref, out_ref
):
    mix, cos_turn, sin_turn = mix_ref[...], cos_ref[...], sin_ref[...]
    inv_mix = inv_mix_ref[...]
    wide = CG * KH
    taps = spectra([block(rows_ref, part, 2 * CG) for part in range(CG)], mix, cos_turn, sin_turn, full_ref)
    taps_re, taps_im = taps[:, :BLK], taps[:, BLK:]
    for seq in range(CG):
        rows = slice(seq * wide, (seq + 1) * wide)
        gated_re, gated_im = gated_ref[rows, :BLK], gated_ref[rows, BLK:]
        grad_re, grad_im = grad_ref[rows, :BLK], grad_ref[rows, BLK:]
        conv = jnp.concatenate(
            [taps_re * gated_re - taps_im * gated_im, taps_re * gated_im + taps_im * gated_re], 1
        )
        back = jnp.concatenate(
            [taps_re * grad_re + taps_im * grad_im, taps_re * grad_im - taps_im * grad_re], 1
        )
        timed = positions(jnp.concatenate([conv, back], 0), 2 * CG, inv_mix, cos_turn, sin_turn, inv_full_ref)
        for row in range(2 * CG):
            out_ref[pl.ds(seq * NB * 2 * CG + row, NB, 2 * CG), :] = timed[:, row * BLK : (row + 1) * BLK]


def join_kernel(shares_ref, timed_ref, out_ref):
    peers = CG * NB
    lag = shares_ref[:NB, :] + shares_ref[NB : 2 * NB, :]
    lag = lag + (shares_ref[2 * NB : 3 * NB, :] + shares_ref[3 * NB :, :])
    for row in range(2 * CG):
        out_ref[pl.ds(row, peers, OUT_ROWS), :] = timed_ref[pl.ds(row, peers, 2 * CG), :]
    for seq in range(CG):
        out_ref[pl.ds(seq * NB * OUT_ROWS + 2 * CG, NB, OUT_ROWS), :] = lag


def share_kernel(scale, rows_ref, out_ref):
    lag = rows_ref[pl.ds(2 * CG, BLK, OUT_ROWS), :].T * scale
    for copy in range(CG):
        out_ref[copy * BLK : (copy + 1) * BLK, :] = lag


def finish_kernel(rows_ref, query_ref, key_ref, value_ref, grad_ref, conv_out_ref, gq_ref, gk_ref, gv_ref):
    for part in range(CG):
        lanes = slice(part * BLK, (part + 1) * BLK)
        conv_s = rows_ref[pl.ds(part, BLK, OUT_ROWS), :].T
        grad_z = rows_ref[pl.ds(CG + part, BLK, OUT_ROWS), :].T
        conv_out_ref[0, :, lanes] = (query_ref[0, :, lanes].astype(jnp.float32) * conv_s).astype(jnp.bfloat16)
        gq_ref[0, :, lanes] = (grad_ref[0, :, lanes].astype(jnp.float32) * conv_s).astype(jnp.bfloat16)
        gk_ref[0, :, lanes] = (grad_z * value_ref[0, :, lanes].astype(jnp.float32)).astype(jnp.bfloat16)
        gv_ref[0, :, lanes] = (grad_z * key_ref[0, :, lanes].astype(jnp.float32)).astype(jnp.bfloat16)


def spread_kernel(parts_ref, out_ref):
    for part in range(CG):
        out_ref[:, part * BLK : (part + 1) * BLK] = parts_ref[part * BLK : (part + 1) * BLK, :]


def call(kernel, out_shape, count, space=VMEM, params=PARAMS, **kwargs):
    single = not isinstance(out_shape, (tuple, list))
    return pl.pallas_call(
        kernel,
        out_shape=out_shape,
        in_specs=[space] * count,
        out_specs=VMEM if single else [VMEM] * len(out_shape),
        compiler_params=params,
        **kwargs,
    )


def f32(*shape):
    return jax.ShapeDtypeStruct(shape, jnp.float32)


def exchange(rows, per):
    peers = CG * NB
    moved = lax.all_to_all(rows.reshape(peers, per, 1, BLK), ("zl", "ctx"), 0, 0, tiled=True)
    return moved.reshape(peers * per, BLK)


def across_y(rows):
    moved = lax.all_to_all(rows.reshape(4, -1, BLK), "y", 0, 0, tiled=True)
    return moved.reshape(rows.shape)


def local(queries, keys, values, grad_out, filter_taps):
    forward_mix, inverse_mix, cos_turn, sin_turn, forward_full, inverse_full = (
        jnp.asarray(t) for t in tables()
    )
    peers = CG * NB
    wide = CG * CG * KH
    scratch = [pltpu.VMEM(queries.shape, jnp.bfloat16)] * 4 + [
        pltpu.VMEM((BLK, BLK), jnp.float32),
        pltpu.SemaphoreType.DMA((5,)),
    ]
    sent = call(send_kernel, f32(peers * IN_ROWS, BLK), 5, HBM, SMALL, scratch_shapes=scratch)(
        *(pltpu.with_memory_space_constraint(a, pltpu.HBM) for a in (queries, keys, values, grad_out, filter_taps))
    )
    rows = exchange(sent, IN_ROWS)
    gated, grad, lag = call(forward_kernel, (f32(wide, 2 * BLK), f32(wide, 2 * BLK), f32(peers, BLK)), 7)(
        rows, forward_mix, cos_turn, sin_turn, forward_full, inverse_mix, inverse_full
    )
    shares = across_y(lag)
    timed = call(inverse_kernel, f32(peers * 2 * CG, BLK), 9)(
        rows, gated, grad, forward_mix, cos_turn, sin_turn, forward_full, inverse_mix, inverse_full
    )
    joined = call(join_kernel, f32(peers * OUT_ROWS, BLK), 2)(shares, timed)
    returned = exchange(joined, OUT_ROWS)
    scale = 1.0 / math.sqrt(16 * NB * BLK)
    spread = across_y(call(functools.partial(share_kernel, scale), f32(CG * BLK, BLK), 1)(returned))
    shape = jax.ShapeDtypeStruct(queries.shape, jnp.bfloat16)
    products = call(finish_kernel, (shape, shape, shape, shape), 5)(returned, queries, keys, values, grad_out)
    return (*products, call(spread_kernel, f32(*filter_taps.shape), 1)(spread))


def solution(mesh):
    split_mesh = Mesh(mesh.devices.reshape(4, 4, 32), ("y", "zl", "ctx"))
    whole = P(("y", "zl"), "ctx", None)
    return jax.shard_map(
        local,
        mesh=split_mesh,
        in_specs=(whole, whole, whole, whole, P("ctx", None)),
        out_specs=(whole, whole, whole, whole, P("ctx", None)),
        check_vma=False,
    )
```

```python
import math

import jax
import jax.numpy as jnp
import ml_dtypes
import numpy as np
from jax import lax
from jax.experimental import pallas as pl
from jax.experimental.pallas import tpu as pltpu
from jax.sharding import Mesh
from jax.sharding import PartitionSpec as P

BLK = 128
NB = 32
CG = 4
KH = 40
IN_ROWS = 2 * CG + 1
OUT_ROWS = 3 * CG
PERIOD = 2 * NB * BLK
VMEM = pl.BlockSpec(memory_space=pltpu.VMEM)
HBM = pl.BlockSpec(memory_space=pltpu.HBM)
SMALL = pltpu.CompilerParams(vmem_limit_bytes=8 * 1024 * 1024)
PARAMS = pltpu.CompilerParams(vmem_limit_bytes=40 * 1024 * 1024)


def high_low(table):
    high = table.astype(ml_dtypes.bfloat16)
    low = (table - high.astype(np.float64)).astype(ml_dtypes.bfloat16)
    return high, low


def tables():
    k1 = np.arange(KH)
    used = (k1 <= NB)[:, None]
    block = np.arange(NB)
    angle = 2.0 * np.pi * ((k1[:, None] * block[None, :]) % (2 * NB)) / (2 * NB)
    mix = np.concatenate([np.cos(angle) * used, -np.sin(angle) * used], 0)
    high, low = high_low(mix)
    forward_mix = np.concatenate([high, high, low], 1)
    weight = np.where((k1 == 0) | (k1 == NB), 1.0, 2.0)[:, None] * used / PERIOD
    back = np.concatenate([np.cos(angle) * weight, -np.sin(angle) * weight], 0).T
    high, low = high_low(back)
    inverse_mix = np.concatenate([high, high, low], 1)
    offset = np.arange(BLK)
    turn = 2.0 * np.pi * (k1[:, None] * offset[None, :]) / PERIOD
    cos_turn = (np.cos(turn) * used).astype(np.float32)
    sin_turn = (np.sin(turn) * used).astype(np.float32)
    full = 2.0 * np.pi * ((offset[:, None] * offset[None, :]) % BLK) / BLK
    cos, sin = np.cos(full), np.sin(full)
    high, low = high_low(np.block([[cos, -sin], [sin, cos]]))
    forward_full = np.concatenate([high, high, low], 0)
    high, low = high_low(np.block([[cos, sin], [-sin, cos]]))
    inverse_full = np.concatenate([high, high, low], 0)
    return forward_mix, inverse_mix, cos_turn, sin_turn, forward_full, inverse_full


def split(value):
    high = value.astype(jnp.bfloat16)
    low = (value - high.astype(jnp.float32)).astype(jnp.bfloat16)
    return high, low


def dot(left, right):
    return jnp.dot(left, right, preferred_element_type=jnp.float32)


def mix_rows(table, operand):
    high, low = split(operand)
    return dot(table, jnp.concatenate([high, low, high], 0))


def full_transform(operand, table_ref):
    high, low = split(operand)
    return dot(jnp.concatenate([high, low, high], 1), table_ref[...])


def spectra(blocks, mix, cos_turn, sin_turn, full_ref):
    mixed = mix_rows(mix, jnp.concatenate(blocks, 1))
    turned = []
    for index in range(len(blocks)):
        lanes = slice(index * BLK, (index + 1) * BLK)
        real, imag = mixed[:KH, lanes], mixed[KH:, lanes]
        turned.append(
            jnp.concatenate(
                [real * cos_turn + imag * sin_turn, imag * cos_turn - real * sin_turn], 1
            )
        )
    return full_transform(jnp.concatenate(turned, 0), full_ref)


def positions(spectrum, count, mix, cos_turn, sin_turn, full_ref):
    back = full_transform(spectrum, full_ref)
    columns = []
    for index in range(count):
        rows = slice(index * KH, (index + 1) * KH)
        real, imag = back[rows, :BLK], back[rows, BLK:]
        columns.append(
            jnp.concatenate(
                [real * cos_turn - imag * sin_turn, imag * cos_turn + real * sin_turn], 0
            )
        )
    return mix_rows(mix, jnp.concatenate(columns, 1))


def send_kernel(query_ref, key_ref, value_ref, grad_ref, taps_ref, out_ref, query, key, value, grad, taps, sems):
    group = lax.axis_index("zl")
    own = taps_ref.at[:, pl.ds(pl.multiple_of(group * BLK, BLK), BLK)]
    pairs = ((key_ref, key), (value_ref, value), (grad_ref, grad), (query_ref, query), (own, taps))
    copies = [pltpu.make_async_copy(src, dst, sems.at[index]) for index, (src, dst) in enumerate(pairs)]
    for copy in copies:
        copy.start()
    copies[0].wait()
    copies[1].wait()
    for part in range(CG):
        lanes = slice(part * BLK, (part + 1) * BLK)
        gated = key[0, :, lanes].astype(jnp.float32) * value[0, :, lanes].astype(jnp.float32)
        out_ref[pl.ds(part, BLK, IN_ROWS), :] = gated.T
    copies[2].wait()
    copies[3].wait()
    for part in range(CG):
        lanes = slice(part * BLK, (part + 1) * BLK)
        grad_s = grad[0, :, lanes].astype(jnp.float32) * query[0, :, lanes].astype(jnp.float32)
        out_ref[pl.ds(CG + part, BLK, IN_ROWS), :] = grad_s.T
    copies[4].wait()
    out_ref[pl.ds(2 * CG, BLK, IN_ROWS), :] = taps[...].T


def block(rows_ref, seq, row):
    return rows_ref[pl.ds(seq * NB * IN_ROWS + row, NB, IN_ROWS), :]


def forward_kernel(
    rows_ref, mix_ref, cos_ref, sin_ref, full_ref, inv_mix_ref, inv_full_ref, gated_ref, grad_ref, lag_ref
):
    mix, cos_turn, sin_turn = mix_ref[...], cos_ref[...], sin_ref[...]
    wide = CG * KH
    lag = None
    for seq in range(CG):
        blocks = [block(rows_ref, seq, row) for row in range(2 * CG)]
        both = spectra(blocks, mix, cos_turn, sin_turn, full_ref)
        rows = slice(seq * wide, (seq + 1) * wide)
        gated_ref[rows, :] = both[:wide]
        grad_ref[rows, :] = both[wide:]
        gated_re, gated_im = both[:wide, :BLK], both[:wide, BLK:]
        grad_re, grad_im = both[wide:, :BLK], both[wide:, BLK:]
        term = jnp.concatenate(
            [grad_re * gated_re + grad_im * gated_im, grad_im * gated_re - grad_re * gated_im], 1
        )
        lag = term if lag is None else lag + term
    timed = positions(lag, CG, inv_mix_ref[...], cos_turn, sin_turn, inv_full_ref)
    for copy in range(4):
        for part in range(CG):
            first = (copy * CG + part) * NB
            lag_ref[first : first + NB, :] = timed[:, part * BLK : (part + 1) * BLK]


def inverse_kernel(
    rows_ref, gated_ref, grad_ref, mix_ref, cos_ref, sin_ref, full_ref, inv_mix_ref, inv_full_ref, out_ref
):
    mix, cos_turn, sin_turn = mix_ref[...], cos_ref[...], sin_ref[...]
    inv_mix = inv_mix_ref[...]
    wide = CG * KH
    taps = spectra([block(rows_ref, part, 2 * CG) for part in range(CG)], mix, cos_turn, sin_turn, full_ref)
    taps_re, taps_im = taps[:, :BLK], taps[:, BLK:]
    for seq in range(CG):
        rows = slice(seq * wide, (seq + 1) * wide)
        gated_re, gated_im = gated_ref[rows, :BLK], gated_ref[rows, BLK:]
        grad_re, grad_im = grad_ref[rows, :BLK], grad_ref[rows, BLK:]
        conv = jnp.concatenate(
            [taps_re * gated_re - taps_im * gated_im, taps_re * gated_im + taps_im * gated_re], 1
        )
        back = jnp.concatenate(
            [taps_re * grad_re + taps_im * grad_im, taps_re * grad_im - taps_im * grad_re], 1
        )
        timed = positions(jnp.concatenate([conv, back], 0), 2 * CG, inv_mix, cos_turn, sin_turn, inv_full_ref)
        for row in range(2 * CG):
            out_ref[pl.ds(seq * NB * 2 * CG + row, NB, 2 * CG), :] = timed[:, row * BLK : (row + 1) * BLK]


def join_kernel(shares_ref, timed_ref, out_ref):
    peers = CG * NB
    lag = shares_ref[:peers, :] + shares_ref[peers : 2 * peers, :]
    lag = lag + (shares_ref[2 * peers : 3 * peers, :] + shares_ref[3 * peers :, :])
    for row in range(2 * CG):
        out_ref[pl.ds(row, peers, OUT_ROWS), :] = timed_ref[pl.ds(row, peers, 2 * CG), :]
    for seq in range(CG):
        for part in range(CG):
            first = seq * NB * OUT_ROWS + 2 * CG + part
            out_ref[pl.ds(first, NB, OUT_ROWS), :] = lag[part * NB : (part + 1) * NB, :]


def finish_kernel(
    scale, rows_ref, query_ref, key_ref, value_ref, grad_ref, conv_out_ref, gq_ref, gk_ref, gv_ref, gf_ref
):
    for part in range(CG):
        lanes = slice(part * BLK, (part + 1) * BLK)
        conv_s = rows_ref[pl.ds(part, BLK, OUT_ROWS), :].T
        grad_z = rows_ref[pl.ds(CG + part, BLK, OUT_ROWS), :].T
        lag = rows_ref[pl.ds(2 * CG + part, BLK, OUT_ROWS), :].T
        conv_out_ref[0, :, lanes] = (query_ref[0, :, lanes].astype(jnp.float32) * conv_s).astype(jnp.bfloat16)
        gq_ref[0, :, lanes] = (grad_ref[0, :, lanes].astype(jnp.float32) * conv_s).astype(jnp.bfloat16)
        gk_ref[0, :, lanes] = (grad_z * value_ref[0, :, lanes].astype(jnp.float32)).astype(jnp.bfloat16)
        gv_ref[0, :, lanes] = (grad_z * key_ref[0, :, lanes].astype(jnp.float32)).astype(jnp.bfloat16)
        gf_ref[:, lanes] = lag * scale


def call(kernel, out_shape, count, space=VMEM, params=PARAMS, **kwargs):
    single = not isinstance(out_shape, (tuple, list))
    return pl.pallas_call(
        kernel,
        out_shape=out_shape,
        in_specs=[space] * count,
        out_specs=VMEM if single else [VMEM] * len(out_shape),
        compiler_params=params,
        **kwargs,
    )


def f32(*shape):
    return jax.ShapeDtypeStruct(shape, jnp.float32)


def exchange(rows, per):
    peers = CG * NB
    moved = lax.all_to_all(rows.reshape(peers, per, 1, BLK), ("zl", "ctx"), 0, 0, tiled=True)
    return moved.reshape(peers * per, BLK)


def local(queries, keys, values, grad_out, filter_taps):
    forward_mix, inverse_mix, cos_turn, sin_turn, forward_full, inverse_full = (
        jnp.asarray(t) for t in tables()
    )
    peers = CG * NB
    wide = CG * CG * KH
    scratch = [pltpu.VMEM(queries.shape, jnp.bfloat16)] * 4 + [
        pltpu.VMEM((BLK, BLK), jnp.float32),
        pltpu.SemaphoreType.DMA((5,)),
    ]
    sent = call(send_kernel, f32(peers * IN_ROWS, BLK), 5, HBM, SMALL, scratch_shapes=scratch)(
        *(pltpu.with_memory_space_constraint(a, pltpu.HBM) for a in (queries, keys, values, grad_out, filter_taps))
    )
    rows = exchange(sent, IN_ROWS)
    gated, grad, lag = call(forward_kernel, (f32(wide, 2 * BLK), f32(wide, 2 * BLK), f32(4 * peers, BLK)), 7)(
        rows, forward_mix, cos_turn, sin_turn, forward_full, inverse_mix, inverse_full
    )
    shares = lax.all_to_all(lag.reshape(4, peers, BLK), "y", 0, 0, tiled=True).reshape(4 * peers, BLK)
    timed = call(inverse_kernel, f32(peers * 2 * CG, BLK), 9)(
        rows, gated, grad, forward_mix, cos_turn, sin_turn, forward_full, inverse_mix, inverse_full
    )
    joined = call(join_kernel, f32(peers * OUT_ROWS, BLK), 2)(shares, timed)
    returned = exchange(joined, OUT_ROWS)
    scale = 1.0 / math.sqrt(16 * NB * BLK)
    shape = jax.ShapeDtypeStruct(queries.shape, jnp.bfloat16)

    def finish(*refs):
        finish_kernel(scale, *refs)

    return tuple(
        call(finish, (shape, shape, shape, shape, f32(*filter_taps.shape)), 5)(
            returned, queries, keys, values, grad_out
        )
    )


def solution(mesh):
    split_mesh = Mesh(mesh.devices.reshape(4, 4, 32), ("y", "zl", "ctx"))
    whole = P(("y", "zl"), "ctx", None)
    return jax.shard_map(
        local,
        mesh=split_mesh,
        in_specs=(whole, whole, whole, whole, P("ctx", None)),
        out_specs=(whole, whole, whole, whole, P("ctx", None)),
        check_vma=False,
    )
```

```python
import math

import jax
import jax.numpy as jnp
import ml_dtypes
import numpy as np
from jax import lax
from jax.experimental import pallas as pl
from jax.experimental.pallas import tpu as pltpu
from jax.sharding import Mesh
from jax.sharding import PartitionSpec as P

BLK = 128
NB = 32
CG = 4
TILE = 8
IN_ROWS = 2 * CG + 1
OUT_ROWS = 3 * CG
PERIOD = 2 * NB * BLK
SPAN = 2 * CG * NB + TILE
VMEM = pl.BlockSpec(memory_space=pltpu.VMEM)
HBM = pl.BlockSpec(memory_space=pltpu.HBM)
SMALL = pltpu.CompilerParams(vmem_limit_bytes=8 * 1024 * 1024)
PARAMS = pltpu.CompilerParams(vmem_limit_bytes=40 * 1024 * 1024)


def high_low(table):
    high = table.astype(ml_dtypes.bfloat16)
    low = (table - high.astype(np.float64)).astype(ml_dtypes.bfloat16)
    return high, low


def tables():
    k1 = np.arange(NB)
    block = np.arange(NB)
    angle = 2.0 * np.pi * ((k1[:, None] * block[None, :]) % (2 * NB)) / (2 * NB)
    last = np.tile(1.0 - 2.0 * (block % 2), (TILE, 1))
    high, low = high_low(np.concatenate([np.cos(angle), -np.sin(angle), last], 0))
    forward_mix = np.concatenate([high, high, low], 1)
    weight = np.where(k1 == 0, 1.0, 2.0)[:, None] / PERIOD
    back = np.concatenate([np.cos(angle) * weight, -np.sin(angle) * weight, last / PERIOD, 0.0 * last], 0).T
    high, low = high_low(back)
    inverse_mix = np.concatenate([high, high, low], 1)
    offset = np.arange(BLK)
    harmonic = np.concatenate([k1, np.full(TILE, NB)])
    turn = 2.0 * np.pi * (harmonic[:, None] * offset[None, :]) / PERIOD
    cos_turn = np.cos(turn).astype(np.float32)
    sin_turn = np.sin(turn).astype(np.float32)
    full = 2.0 * np.pi * ((offset[:, None] * offset[None, :]) % BLK) / BLK
    cos, sin = np.cos(full), np.sin(full)
    high, low = high_low(np.block([[cos, -sin], [sin, cos]]))
    forward_full = np.concatenate([high, high, low], 0)
    high, low = high_low(np.block([[cos, sin], [-sin, cos]]))
    inverse_full = np.concatenate([high, high, low], 0)
    return forward_mix, inverse_mix, cos_turn, sin_turn, forward_full, inverse_full


def split(value):
    high = value.astype(jnp.bfloat16)
    low = (value - high.astype(jnp.float32)).astype(jnp.bfloat16)
    return high, low


def dot(left, right):
    return jnp.dot(left, right, preferred_element_type=jnp.float32)


def mix_rows(table, operand):
    high, low = split(operand)
    return dot(table, jnp.concatenate([high, low, high], 0))


def full_transform(operand, table_ref):
    high, low = split(operand)
    return dot(jnp.concatenate([high, low, high], 1), table_ref[...])


def tile_row():
    return lax.broadcasted_iota(jnp.int32, (TILE, BLK), 0)


def spectra(blocks, mix, cos_turn, sin_turn, full_ref):
    mixed = mix_rows(mix, jnp.concatenate(blocks, 1))
    cos, sin = cos_turn[:NB], sin_turn[:NB]
    turned = []
    last = jnp.zeros((TILE, BLK), jnp.float32)
    own = tile_row() % len(blocks)
    for index in range(len(blocks)):
        lanes = slice(index * BLK, (index + 1) * BLK)
        real, imag = mixed[:NB, lanes], mixed[NB : 2 * NB, lanes]
        turned.append(jnp.concatenate([real * cos + imag * sin, imag * cos - real * sin], 1))
        last = jnp.where(own == index, mixed[2 * NB :, lanes], last)
    turned.append(jnp.concatenate([last * cos_turn[NB:], -last * sin_turn[NB:]], 1))
    return full_transform(jnp.concatenate(turned, 0), full_ref)


def positions(spectrum, count, mix, cos_turn, sin_turn, full_ref):
    back = full_transform(spectrum, full_ref)
    cos, sin = cos_turn[:NB], sin_turn[:NB]
    last = back[count * NB :, :BLK] * cos_turn[NB:] - back[count * NB :, BLK:] * sin_turn[NB:]
    own = tile_row()
    empty = jnp.zeros((TILE, BLK), jnp.float32)
    columns = []
    for index in range(count):
        rows = slice(index * NB, (index + 1) * NB)
        real, imag = back[rows, :BLK], back[rows, BLK:]
        columns.append(
            jnp.concatenate(
                [real * cos - imag * sin, imag * cos + real * sin, jnp.where(own == index, last, empty), empty], 0
            )
        )
    return mix_rows(mix, jnp.concatenate(columns, 1))


def send_kernel(query_ref, key_ref, value_ref, grad_ref, taps_ref, out_ref, query, key, value, grad, taps, sems):
    group = lax.axis_index("zl")
    own = taps_ref.at[:, pl.ds(pl.multiple_of(group * BLK, BLK), BLK)]
    pairs = ((key_ref, key), (value_ref, value), (grad_ref, grad), (query_ref, query), (own, taps))
    copies = [pltpu.make_async_copy(src, dst, sems.at[index]) for index, (src, dst) in enumerate(pairs)]
    for copy in copies:
        copy.start()
    copies[0].wait()
    copies[1].wait()
    for part in range(CG):
        lanes = slice(part * BLK, (part + 1) * BLK)
        gated = key[0, :, lanes].astype(jnp.float32) * value[0, :, lanes].astype(jnp.float32)
        out_ref[pl.ds(part, BLK, IN_ROWS), :] = gated.T
    copies[2].wait()
    copies[3].wait()
    for part in range(CG):
        lanes = slice(part * BLK, (part + 1) * BLK)
        grad_s = grad[0, :, lanes].astype(jnp.float32) * query[0, :, lanes].astype(jnp.float32)
        out_ref[pl.ds(CG + part, BLK, IN_ROWS), :] = grad_s.T
    copies[4].wait()
    out_ref[pl.ds(2 * CG, BLK, IN_ROWS), :] = taps[...].T


def block(rows_ref, seq, row):
    return rows_ref[pl.ds(seq * NB * IN_ROWS + row, NB, IN_ROWS), :]


def forward_kernel(rows_ref, mix_ref, cos_ref, sin_ref, full_ref, inv_mix_ref, inv_full_ref, both_ref, lag_ref):
    mix, cos_turn, sin_turn = mix_ref[...], cos_ref[...], sin_ref[...]
    wide = CG * NB
    lag = None
    for seq in range(CG):
        blocks = [block(rows_ref, seq, row) for row in range(2 * CG)]
        both = spectra(blocks, mix, cos_turn, sin_turn, full_ref)
        both_ref[seq * SPAN : (seq + 1) * SPAN, :] = both
        last = both[2 * wide :]
        gated = jnp.concatenate([both[:wide], last], 0)
        grad = jnp.concatenate([both[wide : 2 * wide], last[CG:], last[:CG]], 0)
        gated_re, gated_im = gated[:, :BLK], gated[:, BLK:]
        grad_re, grad_im = grad[:, :BLK], grad[:, BLK:]
        term = jnp.concatenate(
            [grad_re * gated_re + grad_im * gated_im, grad_im * gated_re - grad_re * gated_im], 1
        )
        lag = term if lag is None else lag + term
    timed = positions(lag, CG, inv_mix_ref[...], cos_turn, sin_turn, inv_full_ref)
    for copy in range(4):
        for part in range(CG):
            first = (copy * CG + part) * NB
            lag_ref[first : first + NB, :] = timed[:, part * BLK : (part + 1) * BLK]


def inverse_kernel(
    rows_ref, both_ref, mix_ref, cos_ref, sin_ref, full_ref, inv_mix_ref, inv_full_ref, out_ref
):
    mix, cos_turn, sin_turn = mix_ref[...], cos_ref[...], sin_ref[...]
    inv_mix = inv_mix_ref[...]
    wide = CG * NB
    taps = spectra([block(rows_ref, part, 2 * CG) for part in range(CG)], mix, cos_turn, sin_turn, full_ref)
    low_im, last_im = taps[:wide, BLK:], taps[wide:, BLK:]
    taps_re = jnp.concatenate([taps[:wide, :BLK], taps[:wide, :BLK], taps[wide:, :BLK]], 0)
    taps_im = jnp.concatenate([low_im, -low_im, jnp.where(tile_row() < CG, last_im, -last_im)], 0)
    for seq in range(CG):
        rows = slice(seq * SPAN, (seq + 1) * SPAN)
        real, imag = both_ref[rows, :BLK], both_ref[rows, BLK:]
        product = jnp.concatenate([taps_re * real - taps_im * imag, taps_re * imag + taps_im * real], 1)
        timed = positions(product, 2 * CG, inv_mix, cos_turn, sin_turn, inv_full_ref)
        for row in range(2 * CG):
            out_ref[pl.ds(seq * NB * 2 * CG + row, NB, 2 * CG), :] = timed[:, row * BLK : (row + 1) * BLK]


def join_kernel(shares_ref, timed_ref, out_ref):
    peers = CG * NB
    lag = shares_ref[:peers, :] + shares_ref[peers : 2 * peers, :]
    lag = lag + (shares_ref[2 * peers : 3 * peers, :] + shares_ref[3 * peers :, :])
    for row in range(2 * CG):
        out_ref[pl.ds(row, peers, OUT_ROWS), :] = timed_ref[pl.ds(row, peers, 2 * CG), :]
    for seq in range(CG):
        for part in range(CG):
            first = seq * NB * OUT_ROWS + 2 * CG + part
            out_ref[pl.ds(first, NB, OUT_ROWS), :] = lag[part * NB : (part + 1) * NB, :]


def finish_kernel(scale, rows_ref, query_ref, key_ref, value_ref, grad_ref, *refs):
    results, (conv_out, gq, gk, gv, gf, sems) = refs[:5], refs[5:]
    held = (conv_out, gq, gk, gv, gf)
    copies = [pltpu.make_async_copy(held[index], results[index], sems.at[index]) for index in range(5)]

    def column(row):
        return rows_ref[pl.ds(row, BLK, OUT_ROWS), :].T

    for part in range(CG):
        gf[:, part * BLK : (part + 1) * BLK] = column(2 * CG + part) * scale
    copies[4].start()
    for part in range(CG):
        lanes = slice(part * BLK, (part + 1) * BLK)
        conv_s = column(part)
        conv_out[0, :, lanes] = (query_ref[0, :, lanes].astype(jnp.float32) * conv_s).astype(jnp.bfloat16)
        gq[0, :, lanes] = (grad_ref[0, :, lanes].astype(jnp.float32) * conv_s).astype(jnp.bfloat16)
    copies[0].start()
    copies[1].start()
    for part in range(CG):
        lanes = slice(part * BLK, (part + 1) * BLK)
        grad_z = column(CG + part)
        gk[0, :, lanes] = (grad_z * value_ref[0, :, lanes].astype(jnp.float32)).astype(jnp.bfloat16)
        gv[0, :, lanes] = (grad_z * key_ref[0, :, lanes].astype(jnp.float32)).astype(jnp.bfloat16)
    copies[2].start()
    copies[3].start()
    for copy in copies:
        copy.wait()


def call(kernel, out_shape, count, space=VMEM, params=PARAMS, out_space=VMEM, **kwargs):
    single = not isinstance(out_shape, (tuple, list))
    return pl.pallas_call(
        kernel,
        out_shape=out_shape,
        in_specs=[space] * count,
        out_specs=out_space if single else [out_space] * len(out_shape),
        compiler_params=params,
        **kwargs,
    )


def f32(*shape):
    return jax.ShapeDtypeStruct(shape, jnp.float32)


def exchange(rows, per):
    peers = CG * NB
    moved = lax.all_to_all(rows.reshape(peers, per, 1, BLK), ("zl", "ctx"), 0, 0, tiled=True)
    return moved.reshape(peers * per, BLK)


def local(queries, keys, values, grad_out, filter_taps):
    forward_mix, inverse_mix, cos_turn, sin_turn, forward_full, inverse_full = (
        jnp.asarray(t) for t in tables()
    )
    peers = CG * NB
    scratch = [pltpu.VMEM(queries.shape, jnp.bfloat16)] * 4 + [
        pltpu.VMEM((BLK, BLK), jnp.float32),
        pltpu.SemaphoreType.DMA((5,)),
    ]
    sent = call(send_kernel, f32(peers * IN_ROWS, BLK), 5, HBM, SMALL, scratch_shapes=scratch)(
        *(pltpu.with_memory_space_constraint(a, pltpu.HBM) for a in (queries, keys, values, grad_out, filter_taps))
    )
    rows = exchange(sent, IN_ROWS)
    both, lag = call(forward_kernel, (f32(CG * SPAN, 2 * BLK), f32(4 * peers, BLK)), 7)(
        rows, forward_mix, cos_turn, sin_turn, forward_full, inverse_mix, inverse_full
    )
    shares = lax.all_to_all(lag.reshape(4, peers, BLK), "y", 0, 0, tiled=True).reshape(4 * peers, BLK)
    timed = call(inverse_kernel, f32(peers * 2 * CG, BLK), 8)(
        rows, both, forward_mix, cos_turn, sin_turn, forward_full, inverse_mix, inverse_full
    )
    joined = call(join_kernel, f32(peers * OUT_ROWS, BLK), 2)(shares, timed)
    returned = exchange(joined, OUT_ROWS)
    scale = 1.0 / math.sqrt(16 * NB * BLK)
    shape = jax.ShapeDtypeStruct(queries.shape, jnp.bfloat16)

    taps_shape = f32(*filter_taps.shape)
    held = [pltpu.VMEM(shape.shape, jnp.bfloat16)] * 4 + [pltpu.VMEM(taps_shape.shape, jnp.float32)]

    def finish(*refs):
        finish_kernel(scale, *refs)

    return tuple(
        call(
            finish,
            (shape, shape, shape, shape, taps_shape),
            5,
            out_space=HBM,
            scratch_shapes=[*held, pltpu.SemaphoreType.DMA((5,))],
        )(returned, queries, keys, values, grad_out)
    )


def solution(mesh):
    split_mesh = Mesh(mesh.devices.reshape(4, 4, 32), ("y", "zl", "ctx"))
    whole = P(("y", "zl"), "ctx", None)
    return jax.shard_map(
        local,
        mesh=split_mesh,
        in_specs=(whole, whole, whole, whole, P("ctx", None)),
        out_specs=(whole, whole, whole, whole, P("ctx", None)),
        check_vma=False,
    )
```

```python
import math

import jax
import jax.numpy as jnp
import ml_dtypes
import numpy as np
from jax import lax
from jax.experimental import pallas as pl
from jax.experimental.pallas import tpu as pltpu
from jax.sharding import Mesh
from jax.sharding import PartitionSpec as P

BLK = 128
NB = 32
CG = 4
TILE = 8
IN_ROWS = 2 * CG + 1
OUT_ROWS = 3 * CG
PERIOD = 2 * NB * BLK
SPAN = 2 * CG * NB + TILE
VMEM = pl.BlockSpec(memory_space=pltpu.VMEM)
HBM = pl.BlockSpec(memory_space=pltpu.HBM)
SMALL = pltpu.CompilerParams(vmem_limit_bytes=8 * 1024 * 1024)
PARAMS = pltpu.CompilerParams(vmem_limit_bytes=40 * 1024 * 1024)


def high_low(table):
    high = table.astype(ml_dtypes.bfloat16)
    low = (table - high.astype(np.float64)).astype(ml_dtypes.bfloat16)
    return high, low


def tables():
    k1 = np.arange(NB)
    block = np.arange(NB)
    angle = 2.0 * np.pi * ((k1[:, None] * block[None, :]) % (2 * NB)) / (2 * NB)
    last = np.tile(1.0 - 2.0 * (block % 2), (TILE, 1))
    high, low = high_low(np.concatenate([np.cos(angle), -np.sin(angle), last], 0))
    forward_mix = np.concatenate([high, high, low], 1)
    weight = np.where(k1 == 0, 1.0, 2.0)[:, None] / PERIOD
    back = np.concatenate([np.cos(angle) * weight, -np.sin(angle) * weight, last / PERIOD, 0.0 * last], 0).T
    high, low = high_low(back)
    inverse_mix = np.concatenate([high, high, low], 1)
    offset = np.arange(BLK)
    harmonic = np.concatenate([k1, np.full(TILE, NB)])
    turn = 2.0 * np.pi * (harmonic[:, None] * offset[None, :]) / PERIOD
    cos_turn = np.cos(turn).astype(np.float32)
    sin_turn = np.sin(turn).astype(np.float32)
    full = 2.0 * np.pi * ((offset[:, None] * offset[None, :]) % BLK) / BLK
    cos, sin = np.cos(full), np.sin(full)
    high, low = high_low(np.block([[cos, -sin], [sin, cos]]))
    forward_full = np.concatenate([high, high, low], 0)
    high, low = high_low(np.block([[cos, sin], [-sin, cos]]))
    inverse_full = np.concatenate([high, high, low], 0)
    return forward_mix, inverse_mix, cos_turn, sin_turn, forward_full, inverse_full


def split(value):
    high = value.astype(jnp.bfloat16)
    low = (value - high.astype(jnp.float32)).astype(jnp.bfloat16)
    return high, low


def dot(left, right):
    return jnp.dot(left, right, preferred_element_type=jnp.float32)


def mix_rows(table, operand):
    high, low = split(operand)
    return dot(table, jnp.concatenate([high, low, high], 0))


def full_transform(operand, table_ref):
    high, low = split(operand)
    return dot(jnp.concatenate([high, low, high], 1), table_ref[...])


def tile_row():
    return lax.broadcasted_iota(jnp.int32, (TILE, BLK), 0)


def spectra(blocks, mix, cos_turn, sin_turn, full_ref):
    mixed = mix_rows(mix, jnp.concatenate(blocks, 1))
    cos, sin = cos_turn[:NB], sin_turn[:NB]
    turned = []
    last = jnp.zeros((TILE, BLK), jnp.float32)
    own = tile_row() % len(blocks)
    for index in range(len(blocks)):
        lanes = slice(index * BLK, (index + 1) * BLK)
        real, imag = mixed[:NB, lanes], mixed[NB : 2 * NB, lanes]
        turned.append(jnp.concatenate([real * cos + imag * sin, imag * cos - real * sin], 1))
        last = jnp.where(own == index, mixed[2 * NB :, lanes], last)
    turned.append(jnp.concatenate([last * cos_turn[NB:], -last * sin_turn[NB:]], 1))
    return full_transform(jnp.concatenate(turned, 0), full_ref)


def positions(spectrum, count, mix, cos_turn, sin_turn, full_ref):
    back = full_transform(spectrum, full_ref)
    cos, sin = cos_turn[:NB], sin_turn[:NB]
    last = back[count * NB :, :BLK] * cos_turn[NB:] - back[count * NB :, BLK:] * sin_turn[NB:]
    own = tile_row()
    empty = jnp.zeros((TILE, BLK), jnp.float32)
    columns = []
    for index in range(count):
        rows = slice(index * NB, (index + 1) * NB)
        real, imag = back[rows, :BLK], back[rows, BLK:]
        columns.append(
            jnp.concatenate(
                [real * cos - imag * sin, imag * cos + real * sin, jnp.where(own == index, last, empty), empty], 0
            )
        )
    return mix_rows(mix, jnp.concatenate(columns, 1))


def send_kernel(query_ref, key_ref, value_ref, grad_ref, taps_ref, out_ref, query, key, value, grad, taps, sems):
    group = lax.axis_index("zl")
    own = taps_ref.at[:, pl.ds(pl.multiple_of(group * BLK, BLK), BLK)]
    pairs = ((key_ref, key), (value_ref, value), (grad_ref, grad), (query_ref, query), (own, taps))
    copies = [pltpu.make_async_copy(src, dst, sems.at[index]) for index, (src, dst) in enumerate(pairs)]
    for copy in copies:
        copy.start()
    copies[0].wait()
    copies[1].wait()
    for part in range(CG):
        lanes = slice(part * BLK, (part + 1) * BLK)
        gated = key[0, :, lanes].astype(jnp.float32) * value[0, :, lanes].astype(jnp.float32)
        out_ref[pl.ds(part, BLK, IN_ROWS), :] = gated.T
    copies[2].wait()
    copies[3].wait()
    for part in range(CG):
        lanes = slice(part * BLK, (part + 1) * BLK)
        grad_s = grad[0, :, lanes].astype(jnp.float32) * query[0, :, lanes].astype(jnp.float32)
        out_ref[pl.ds(CG + part, BLK, IN_ROWS), :] = grad_s.T
    copies[4].wait()
    out_ref[pl.ds(2 * CG, BLK, IN_ROWS), :] = taps[...].T


def block(rows_ref, seq, row):
    return rows_ref[pl.ds(seq * NB * IN_ROWS + row, NB, IN_ROWS), :]


def forward_kernel(rows_ref, mix_ref, cos_ref, sin_ref, full_ref, inv_mix_ref, inv_full_ref, both_ref, lag_ref):
    mix, cos_turn, sin_turn = mix_ref[...], cos_ref[...], sin_ref[...]
    wide = CG * NB
    lag = None
    for seq in range(CG):
        blocks = [block(rows_ref, seq, row) for row in range(2 * CG)]
        both = spectra(blocks, mix, cos_turn, sin_turn, full_ref)
        both_ref[seq * SPAN : (seq + 1) * SPAN, :] = both
        last = both[2 * wide :]
        gated = jnp.concatenate([both[:wide], last], 0)
        grad = jnp.concatenate([both[wide : 2 * wide], last[CG:], last[:CG]], 0)
        gated_re, gated_im = gated[:, :BLK], gated[:, BLK:]
        grad_re, grad_im = grad[:, :BLK], grad[:, BLK:]
        term = jnp.concatenate(
            [grad_re * gated_re + grad_im * gated_im, grad_im * gated_re - grad_re * gated_im], 1
        )
        lag = term if lag is None else lag + term
    timed = positions(lag, CG, inv_mix_ref[...], cos_turn, sin_turn, inv_full_ref)
    for copy in range(4):
        for part in range(CG):
            first = (copy * CG + part) * NB
            lag_ref[first : first + NB, :] = timed[:, part * BLK : (part + 1) * BLK]


def inverse_kernel(
    rows_ref, both_ref, mix_ref, cos_ref, sin_ref, full_ref, inv_mix_ref, inv_full_ref, out_ref
):
    mix, cos_turn, sin_turn = mix_ref[...], cos_ref[...], sin_ref[...]
    inv_mix = inv_mix_ref[...]
    wide = CG * NB
    taps = spectra([block(rows_ref, part, 2 * CG) for part in range(CG)], mix, cos_turn, sin_turn, full_ref)
    low_im, last_im = taps[:wide, BLK:], taps[wide:, BLK:]
    taps_re = jnp.concatenate([taps[:wide, :BLK], taps[:wide, :BLK], taps[wide:, :BLK]], 0)
    taps_im = jnp.concatenate([low_im, -low_im, jnp.where(tile_row() < CG, last_im, -last_im)], 0)
    for seq in range(CG):
        rows = slice(seq * SPAN, (seq + 1) * SPAN)
        real, imag = both_ref[rows, :BLK], both_ref[rows, BLK:]
        product = jnp.concatenate([taps_re * real - taps_im * imag, taps_re * imag + taps_im * real], 1)
        timed = positions(product, 2 * CG, inv_mix, cos_turn, sin_turn, inv_full_ref)
        for row in range(2 * CG):
            out_ref[row * CG * NB + seq * NB : row * CG * NB + (seq + 1) * NB, :] = timed[:, row * BLK : (row + 1) * BLK]


def join_kernel(shares_ref, timed_ref, out_ref):
    peers = CG * NB
    lag = shares_ref[:peers, :] + shares_ref[peers : 2 * peers, :]
    lag = lag + (shares_ref[2 * peers : 3 * peers, :] + shares_ref[3 * peers :, :])
    for row in range(2 * CG):
        out_ref[pl.ds(row, peers, OUT_ROWS), :] = timed_ref[row * peers : (row + 1) * peers, :]
    for seq in range(CG):
        for part in range(CG):
            first = seq * NB * OUT_ROWS + 2 * CG + part
            out_ref[pl.ds(first, NB, OUT_ROWS), :] = lag[part * NB : (part + 1) * NB, :]


def finish_kernel(scale, rows_ref, query_ref, key_ref, value_ref, grad_ref, *refs):
    results, (conv_out, gq, gk, gv, gf, sems) = refs[:5], refs[5:]
    held = (conv_out, gq, gk, gv, gf)
    copies = [pltpu.make_async_copy(held[index], results[index], sems.at[index]) for index in range(5)]

    def column(row):
        return rows_ref[pl.ds(row, BLK, OUT_ROWS), :].T

    for part in range(CG):
        gf[:, part * BLK : (part + 1) * BLK] = column(2 * CG + part) * scale
    copies[4].start()
    for part in range(CG):
        lanes = slice(part * BLK, (part + 1) * BLK)
        conv_s = column(part)
        conv_out[0, :, lanes] = (query_ref[0, :, lanes].astype(jnp.float32) * conv_s).astype(jnp.bfloat16)
        gq[0, :, lanes] = (grad_ref[0, :, lanes].astype(jnp.float32) * conv_s).astype(jnp.bfloat16)
    copies[0].start()
    copies[1].start()
    for part in range(CG):
        lanes = slice(part * BLK, (part + 1) * BLK)
        grad_z = column(CG + part)
        gk[0, :, lanes] = (grad_z * value_ref[0, :, lanes].astype(jnp.float32)).astype(jnp.bfloat16)
        gv[0, :, lanes] = (grad_z * key_ref[0, :, lanes].astype(jnp.float32)).astype(jnp.bfloat16)
    copies[2].start()
    copies[3].start()
    for copy in copies:
        copy.wait()


def call(kernel, out_shape, count, space=VMEM, params=PARAMS, out_space=VMEM, **kwargs):
    single = not isinstance(out_shape, (tuple, list))
    return pl.pallas_call(
        kernel,
        out_shape=out_shape,
        in_specs=[space] * count,
        out_specs=out_space if single else [out_space] * len(out_shape),
        compiler_params=params,
        **kwargs,
    )


def f32(*shape):
    return jax.ShapeDtypeStruct(shape, jnp.float32)


def exchange(rows, per):
    peers = CG * NB
    moved = lax.all_to_all(rows.reshape(peers, per, 1, BLK), ("zl", "ctx"), 0, 0, tiled=True)
    return moved.reshape(peers * per, BLK)


def local(queries, keys, values, grad_out, filter_taps):
    forward_mix, inverse_mix, cos_turn, sin_turn, forward_full, inverse_full = (
        jnp.asarray(t) for t in tables()
    )
    peers = CG * NB
    scratch = [pltpu.VMEM(queries.shape, jnp.bfloat16)] * 4 + [
        pltpu.VMEM((BLK, BLK), jnp.float32),
        pltpu.SemaphoreType.DMA((5,)),
    ]
    sent = call(send_kernel, f32(peers * IN_ROWS, BLK), 5, HBM, SMALL, scratch_shapes=scratch)(
        *(pltpu.with_memory_space_constraint(a, pltpu.HBM) for a in (queries, keys, values, grad_out, filter_taps))
    )
    rows = exchange(sent, IN_ROWS)
    both, lag = call(forward_kernel, (f32(CG * SPAN, 2 * BLK), f32(4 * peers, BLK)), 7)(
        rows, forward_mix, cos_turn, sin_turn, forward_full, inverse_mix, inverse_full
    )
    shares = lax.all_to_all(lag.reshape(4, peers, BLK), "y", 0, 0, tiled=True).reshape(4 * peers, BLK)
    timed = call(inverse_kernel, f32(peers * 2 * CG, BLK), 8)(
        rows, both, forward_mix, cos_turn, sin_turn, forward_full, inverse_mix, inverse_full
    )
    joined = call(join_kernel, f32(peers * OUT_ROWS, BLK), 2)(shares, timed)
    returned = exchange(joined, OUT_ROWS)
    scale = 1.0 / math.sqrt(16 * NB * BLK)
    shape = jax.ShapeDtypeStruct(queries.shape, jnp.bfloat16)

    taps_shape = f32(*filter_taps.shape)
    held = [pltpu.VMEM(shape.shape, jnp.bfloat16)] * 4 + [pltpu.VMEM(taps_shape.shape, jnp.float32)]

    def finish(*refs):
        finish_kernel(scale, *refs)

    return tuple(
        call(
            finish,
            (shape, shape, shape, shape, taps_shape),
            5,
            out_space=HBM,
            scratch_shapes=[*held, pltpu.SemaphoreType.DMA((5,))],
        )(returned, queries, keys, values, grad_out)
    )


def solution(mesh):
    split_mesh = Mesh(mesh.devices.reshape(4, 4, 32), ("y", "zl", "ctx"))
    whole = P(("y", "zl"), "ctx", None)
    return jax.shard_map(
        local,
        mesh=split_mesh,
        in_specs=(whole, whole, whole, whole, P("ctx", None)),
        out_specs=(whole, whole, whole, whole, P("ctx", None)),
        check_vma=False,
    )
```
